32 devices in a mesh: dp: 8 (over z, x), shard: 4 (over y, core).
Axes of the slice: x: 2, y: 2, z: 4, core: 2. Of those that a mesh axis runs over, the one named last changes fastest.
Arguments:
- hidden_in: bfloat16 [32768, 576], P(('dp', 'shard')), may hold values from -6 to 6
- cotangent: bfloat16 [32768, 576], P(('dp', 'shard')), may hold values from -6 to 6
- lengths: int32 [32, 4], P(('dp', 'shard')), may hold values from 1 to 512, 1024 in all within a row
- w_qkv: float32 [576, 960], P('shard'), may hold values from -0.25 to 0.25
- w_out: float32 [576, 576], P('shard'), may hold values from -2 to 2
- w_gu: float32 [576, 3072], P('shard'), may hold values from -0.25 to 0.25
- w_down: float32 [1536, 576], P('shard'), may hold values from -0.15625 to 0.15625
- norm_gains: float32 [2, 576], P(None, 'shard'), may hold values from 0.1 to 1.9
- moment_qkv: float32 [576, 960], P('shard'), may hold values from -0.3 to 0.3
- moment_out: float32 [576, 576], P('shard'), may hold values from -0.3 to 0.3
- moment_gu: float32 [576, 3072], P('shard'), may hold values from -0.3 to 0.3
- moment_down: float32 [1536, 576], P('shard'), may hold values from -0.3 to 0.3
- moment_gains: float32 [2, 576], P(None, 'shard'), may hold values from -0.3 to 0.3
- square_qkv: float32 [576, 960], P('shard'), may hold values from 0.002 to 0.02
- square_out: float32 [576, 576], P('shard'), may hold values from 0.002 to 0.02
- square_gu: float32 [576, 3072], P('shard'), may hold values from 0.002 to 0.02
- square_down: float32 [1536, 576], P('shard'), may hold values from 0.002 to 0.02
- square_gains: float32 [2, 576], P(None, 'shard'), may hold values from 0.002 to 0.02
Outputs:
- output: bfloat16 [32768, 576], P(('dp', 'shard'))
- grad_input: bfloat16 [32768, 576], P(('dp', 'shard'))
- grad_qkv: float32 [576, 960], P('shard')
- grad_out: float32 [576, 576], P('shard')
- grad_gu: float32 [576, 3072], P('shard')
- grad_down: float32 [1536, 576], P('shard')
- grad_gains: float32 [2, 576], P(None, 'shard')
- new_qkv: float32 [576, 960], P('shard')
- new_out: float32 [576, 576], P('shard')
- new_gu: float32 [576, 3072], P('shard')
- new_down: float32 [1536, 576], P('shard')
- new_gains: float32 [2, 576], P(None, 'shard')
- new_moment_qkv: float32 [576, 960], P('shard')
- new_moment_out: float32 [576, 576], P('shard')
- new_moment_gu: float32 [576, 3072], P('shard')
- new_moment_down: float32 [1536, 576], P('shard')
- new_moment_gains: float32 [2, 576], P(None, 'shard')
- new_square_qkv: float32 [576, 960], P('shard')
- new_square_out: float32 [576, 576], P('shard')
- new_square_gu: float32 [576, 3072], P('shard')
- new_square_down: float32 [1536, 576], P('shard')
- new_square_gains: float32 [2, 576], P(None, 'shard')
The draws below stay inside these ranges and needn't reach their ends.
Inputs may be any that keep to these rules, and one draw needn't show every extreme that they name: Each row holds the lengths of one device's sequences; they sum to 1024, and the largest is 512.
All inputs are finite; a program needn't handle non-finite values.
Results may differ from the reference program's by a relative error of at most 0.03.
The reference program's roundings to bfloat16 on the way count: a program that leaves them out, or rounds other values in their place, can miss the bound.
Values may be sent and summed in bfloat16 or wider, within the bound.
No kernel may reach another device: no remote copies, remote signals or barrier semaphores. Data moves between devices by JAX's collectives and lax.ppermute only.
A program may use at most 192 MiB of HBM per device.

```python
import math
import jax
import jax.numpy as jnp
import numpy as np
from jax import lax

D = 576
HEADS = 9
KV_HEADS = 3
HD = 64
FF = 1536
QKV = 960
TOK_DEV = 1024
MOST = 512
SEQS = 4
STEP = 3
TOKENS = 32768
N_DP = 8
N_SHARD = 4


def steps_of(rng, extent, pieces, least, top_value):
    def one(dim, blocks):
        draws = jax.random.uniform(jax.random.fold_in(jax.random.fold_in(rng, 6), dim), (blocks,), jnp.float32, least / len(pieces), top_value / len(pieces))
        return jnp.repeat(jnp.exp(draws), extent[dim] // blocks).reshape((-1,) + (1,) * (len(extent) - dim - 1))

    factor_of = one(*pieces[0])
    for cut in pieces[1:]:
        factor_of = factor_of * one(*cut)
    return factor_of


def profile(amount, total, bound, slope):
    weights = [(1 << 20) // math.isqrt(grade ** slope) + 1 for grade in range(2, amount + 1)]
    spare, holding = total - bound - (amount - 1), [1] * (amount - 1)
    while spare > 0:
        free = [i for i in range(amount - 1) if holding[i] < bound]
        whole, left = sum([weights[i] for i in free]), spare
        for i in free:
            extra = min(bound - holding[i], max(1, left * weights[i] // whole), spare)
            holding[i] = holding[i] + extra
            spare = spare - extra
    return np.array([bound] + holding)


def uneven(key, count, total, limit, skew):
    if count == 2:
        one = jax.random.randint(key, (), max(1, total - limit), min(limit, total - 1) + 1)
        return jnp.stack([one, total - one])
    sizes = jnp.asarray(profile(count, total, limit, skew), jnp.int32)
    pairs = (count - 1) // 2
    giver, taker = sizes[1:1 + 2 * pairs:2], sizes[2:2 + 2 * pairs:2]
    margin = jnp.minimum(giver - 1, limit - taker)
    shifted = jax.random.randint(jax.random.fold_in(key, 1), (pairs,), 0, 1 << 20) % (margin + 1)
    sizes = sizes.at[1:1 + 2 * pairs:2].set(giver - shifted).at[2:2 + 2 * pairs:2].set(taker + shifted)
    return sizes[jax.random.permutation(jax.random.fold_in(key, 2), count)]


def bell_draw(rng, dims, deviation, most, pieces=(), kind=jnp.bfloat16):
    level = steps_of(rng, dims, pieces, -0.22, 0.18) if pieces else 1.0
    drawn = jax.random.normal(rng, dims, jnp.float32) * deviation * level
    return jnp.minimum(jnp.maximum(drawn, -most), most).astype(kind)


def setup_inputs(seed: int = 0) -> dict:
    key_list = jax.random.split(jax.random.key(seed), 19)
    hidden_in = bell_draw(key_list[0], (TOKENS, D), 1.0, 6.0, ((0, 32),))
    cotangent = bell_draw(key_list[1], (TOKENS, D), 1.0, 6.0, ((0, 32),))
    lengths = jax.vmap(lambda own: uneven(own, SEQS, TOK_DEV, MOST, 2))(jax.random.split(key_list[2], (N_DP * N_SHARD))).reshape((N_DP * N_SHARD, SEQS)).astype(jnp.int32)
    w_qkv = bell_draw(key_list[3], (D, QKV), D ** -0.5, 0.25, ((0, 4),), jnp.float32)
    w_out = bell_draw(key_list[4], (D, D), (D // 64) ** -0.5, 2.0, ((0, 4),), jnp.float32)
    w_gu = bell_draw(key_list[5], (D, 2 * FF), D ** -0.5, 0.25, ((0, 4),), jnp.float32)
    w_down = bell_draw(key_list[6], (FF, D), FF ** -0.5, 0.15625, ((0, 4),), jnp.float32)
    norm_gains = jnp.clip(1.0 + 0.18 * jax.random.normal(key_list[7], (2, D), jnp.float32), 0.1, 1.9)
    moment_qkv = bell_draw(key_list[8], (D, QKV), 0.05, 0.3, ((0, 4),), jnp.float32)
    moment_out = bell_draw(key_list[9], (D, D), 0.05, 0.3, ((0, 4),), jnp.float32)
    moment_gu = bell_draw(key_list[10], (D, 2 * FF), 0.05, 0.3, ((0, 4),), jnp.float32)
    moment_down = bell_draw(key_list[11], (FF, D), 0.05, 0.3, ((0, 4),), jnp.float32)
    moment_gains = bell_draw(key_list[12], (2, D), 0.05, 0.3, ((1, 4),), jnp.float32)
    square_qkv = jnp.clip(jnp.exp(math.log(0.02) - 2.30258502 * jax.random.uniform(key_list[13], (D, QKV), jnp.float32) ** steps_of(key_list[13], (D, QKV), ((0, 4),), -0.2, 0.2)), 0.002, 0.02)
    square_out = jnp.clip(jnp.exp(math.log(0.02) - 2.30258502 * jax.random.uniform(key_list[14], (D, D), jnp.float32) ** steps_of(key_list[14], (D, D), ((0, 4),), -0.2, 0.2)), 0.002, 0.02)
    square_gu = jnp.clip(jnp.exp(math.log(0.02) - 2.30258502 * jax.random.uniform(key_list[15], (D, 2 * FF), jnp.float32) ** steps_of(key_list[15], (D, 2 * FF), ((0, 4),), -0.2, 0.2)), 0.002, 0.02)
    square_down = jnp.clip(jnp.exp(math.log(0.02) - 2.30258502 * jax.random.uniform(key_list[16], (FF, D), jnp.float32) ** steps_of(key_list[16], (FF, D), ((0, 4),), -0.2, 0.2)), 0.002, 0.02)
    square_gains = jnp.clip(jnp.exp(math.log(0.02) - 2.30258502 * jax.random.uniform(key_list[17], (2, D), jnp.float32) ** steps_of(key_list[17], (2, D), ((1, 4),), -0.2, 0.2)), 0.002, 0.02)
    return {"hidden_in": hidden_in, "cotangent": cotangent, "lengths": lengths, "w_qkv": w_qkv, "w_out": w_out, "w_gu": w_gu, "w_down": w_down, "norm_gains": norm_gains, "moment_qkv": moment_qkv, "moment_out": moment_out, "moment_gu": moment_gu, "moment_down": moment_down, "moment_gains": moment_gains, "square_qkv": square_qkv, "square_out": square_out, "square_gu": square_gu, "square_down": square_down, "square_gains": square_gains}


eps_norm = 1e-05
rope_base = 100000.0
beta_one = 0.9
beta_two = 0.95
adam_eps = 1e-08
rate_matrix = 0.04
rate_gain = 0.15
decay_weight = 0.1

@jax.custom_vjp
def low(v):
    return lax.optimization_barrier(v.astype(jnp.bfloat16)).astype(jnp.float32)

@jax.custom_vjp
def low_back(v):
    return v

def low_keep(v):
    return (low(v), None)

def low_pass(kept, grad):
    return (grad,)

def back_keep(v):
    return (v, None)

def back_low(kept, grad):
    return (low(grad),)
low.defvjp(low_keep, low_pass)
low_back.defvjp(back_keep, back_low)

def seq_layout(length_row, tokens):
    seq_ends = jnp.cumsum(length_row).astype(jnp.int32)
    token_index = jnp.arange(tokens, dtype=jnp.int32)
    past_end = token_index[:, None] >= seq_ends[None, :]
    segment = lax.optimization_barrier(jnp.sum(past_end.astype(jnp.int32), 1)).astype(jnp.int32)
    seq_start = lax.optimization_barrier(jnp.sum(jnp.where(past_end, length_row[None, :], 0), 1)).astype(jnp.int32)
    return (segment, token_index - seq_start)

def rope_tables(position, width):
    half_width = width // 2
    inverse = rope_base ** (-(jnp.arange(half_width, dtype=jnp.float32) * 2.0) / width)
    angles = position.astype(jnp.float32)[:, None] * inverse[None, :]
    return (jnp.cos(angles), jnp.sin(angles))

def rotate(values, cosine_table, sine_table):
    half_width = values.shape[-1] // 2
    lower_half = values[..., :half_width]
    upper_half = values[..., half_width:]
    return jnp.concatenate([lower_half * cosine_table - upper_half * sine_table, upper_half * cosine_table + lower_half * sine_table], -1)

def rms_norm(values):
    return values * lax.rsqrt(lax.optimization_barrier(jnp.mean(values * values, -1, keepdims=True)) + eps_norm)

def layer(pack_values, length_row, w_qkv, w_out, w_gu, w_down, norm_gains):
    tokens = pack_values.shape[0]
    group_size = HEADS // KV_HEADS
    kv_width = KV_HEADS * HD
    segment, position = seq_layout(length_row, tokens)
    token_index = jnp.arange(tokens, dtype=jnp.int32)
    allowed = (segment[:, None] == segment[None, :]) & (token_index[None, :] <= token_index[:, None])
    cosine_table, sine_table = rope_tables(position, HD)
    input_low = low(rms_norm(pack_values) * norm_gains[0][None, :])
    proj_qkv = low_back(jnp.dot(input_low, w_qkv, precision=lax.Precision.HIGHEST))
    query_low = low(rotate(proj_qkv[:, :D].reshape(tokens, KV_HEADS, group_size, HD), cosine_table[:, None, None, :], sine_table[:, None, None, :]))
    keys_low = low(rotate(proj_qkv[:, D:D + kv_width].reshape(tokens, KV_HEADS, HD), cosine_table[:, None, :], sine_table[:, None, :]))
    values_low = low(proj_qkv[:, D + kv_width:].reshape(tokens, KV_HEADS, HD))
    scores = jnp.einsum('qkgd,tkd->kgqt', query_low, keys_low, precision=lax.Precision.HIGHEST) * HD ** (-0.5)
    scores = low_back(jnp.where(allowed[None, None], scores, -1e+30))
    weights = low(jax.nn.softmax(scores, -1))
    mixed_low = jnp.einsum('kgqt,tkd->qkgd', weights, values_low, precision=lax.Precision.HIGHEST).reshape(tokens, D)
    mixed_low = low(low_back(mixed_low))
    middle = pack_values + low_back(jnp.dot(mixed_low, w_out, precision=lax.Precision.HIGHEST))
    middle_low = low(rms_norm(middle) * norm_gains[1][None, :])
    gate_up = low_back(jnp.dot(middle_low, w_gu, precision=lax.Precision.HIGHEST))
    hidden = low(jax.nn.silu(gate_up[:, :FF]) * gate_up[:, FF:])
    return middle + jnp.dot(hidden, w_down, precision=lax.Precision.HIGHEST)

def adam_update(weight, moment, square, gradient, step_rate, shrink):
    moment_new = beta_one * moment + (1.0 - beta_one) * gradient
    square_new = beta_two * square + (1.0 - beta_two) * gradient * gradient
    mean_hat = moment_new / (1.0 - beta_one ** STEP)
    square_hat = square_new / (1.0 - beta_two ** STEP)
    change = -step_rate * (mean_hat / (jnp.sqrt(square_hat) + adam_eps) + shrink * weight)
    return (change, moment_new, square_new)

def reference(hidden_in, cotangent, lengths, w_qkv, w_out, w_gu, w_down, norm_gains, moment_qkv, moment_out, moment_gu, moment_down, moment_gains, square_qkv, square_out, square_gu, square_down, square_gains):
    devices = N_DP * N_SHARD
    packs = hidden_in.astype(jnp.float32).reshape(devices, TOK_DEV, D)

    def whole(pack_all, wqkv_full, wout_full, wgu_full, wdown_full, gains_full):
        low_qkv = low(wqkv_full)
        low_out = low(wout_full)
        low_gu = low(wgu_full)
        low_down = low(wdown_full)
        low_gains = low(gains_full)

        def one_pack(pack_values, length_row):
            return layer(pack_values, length_row, low_qkv, low_out, low_gu, low_down, low_gains)
        checked = jax.checkpoint(one_pack)
        return lax.map(lambda packed: checked(packed[0], packed[1]), (pack_all, lengths))
    outputs, pull = jax.vjp(whole, packs, w_qkv, w_out, w_gu, w_down, norm_gains)
    grads = pull(cotangent.astype(jnp.float32).reshape(devices, TOK_DEV, D))
    factor = 1.0 / math.sqrt(devices * TOK_DEV)
    grad_qkv = grads[1] * factor
    grad_out = grads[2] * factor
    grad_gu = grads[3] * factor
    grad_down = grads[4] * factor
    grad_gains = grads[5] * factor
    new_qkv, new_moment_qkv, new_square_qkv = adam_update(w_qkv, moment_qkv, square_qkv, grad_qkv, rate_matrix, decay_weight)
    new_out, new_moment_out, new_square_out = adam_update(w_out, moment_out, square_out, grad_out, rate_matrix, decay_weight)
    new_gu, new_moment_gu, new_square_gu = adam_update(w_gu, moment_gu, square_gu, grad_gu, rate_matrix, decay_weight)
    new_down, new_moment_down, new_square_down = adam_update(w_down, moment_down, square_down, grad_down, rate_matrix, decay_weight)
    new_gains, new_moment_gains, new_square_gains = adam_update(norm_gains, moment_gains, square_gains, grad_gains, rate_gain, 0.0)
    output = outputs.reshape(devices * TOK_DEV, D).astype(jnp.bfloat16)
    grad_input = grads[0].reshape(devices * TOK_DEV, D).astype(jnp.bfloat16)
    return (output, grad_input, grad_qkv, grad_out, grad_gu, grad_down, grad_gains, new_qkv, new_out, new_gu, new_down, new_gains, new_moment_qkv, new_moment_out, new_moment_gu, new_moment_down, new_moment_gains, new_square_qkv, new_square_out, new_square_gu, new_square_down, new_square_gains)
```

```python
import functools
import math

import jax
import jax.numpy as jnp
from jax import lax
from jax.experimental import pallas as pl
from jax.experimental.pallas import tpu as pltpu
from jax.sharding import PartitionSpec as P

D = 576
HEADS = 9
KV = 3
GROUP = HEADS // KV
HD = 64
HALF = HD // 2
FF = 1536
QKV = 960
STEP = 3
SHARDS = 4
PIECES = 8
ROWS = D // SHARDS
ROWS_D = FF // SHARDS
DROWS = D // PIECES
TB = 256
WINDOW = 512
LANE = 128
PAD_D = 640
SLAB = ROWS + DROWS
OUT_ROWS = 96

eps_norm = 1e-05
rope_base = 100000.0
beta_one = 0.9
beta_two = 0.95
adam_eps = 1e-08
rate_matrix = 0.04
rate_gain = 0.15
decay_weight = 0.1

f32 = jnp.float32
bf16 = jnp.bfloat16
VM = pl.BlockSpec(memory_space=pltpu.VMEM)
SM = pl.BlockSpec(memory_space=pltpu.SMEM)
ANY = pl.BlockSpec(memory_space=pl.ANY)
PEERS = (0, 2, 1, 3)

OUT_RUNS = []
for _p in range(PIECES):
    _runs, _n = [], 12 * _p
    while _n < 12 * _p + 12 and _n < 90:
        _k, _q = divmod(_n, 18)
        _len = min(18 - _q, 12 * _p + 12 - _n)
        _runs.append(((_n - 12 * _p) * 8, _k, _q * 8, _len * 8))
        _n += _len
    OUT_RUNS.append(_runs)


def nn(a, b):
    return lax.dot_general(a, b, (((1,), (0,)), ((), ())), preferred_element_type=f32)


def nt(a, b):
    return lax.dot_general(a, b, (((1,), (1,)), ((), ())), preferred_element_type=f32)


def call(kernel, outs, in_specs, out_specs, scratch, name, flops, moved, limit=60):
    return pl.pallas_call(
        kernel,
        out_shape=outs,
        in_specs=in_specs,
        out_specs=out_specs,
        scratch_shapes=scratch,
        name=name,
        cost_estimate=pl.CostEstimate(flops=int(flops), bytes_accessed=int(moved), transcendentals=0),
        compiler_params=pltpu.CompilerParams(vmem_limit_bytes=limit * 1024 * 1024),
    )


def sds(shape, dtype):
    return jax.ShapeDtypeStruct(shape, dtype)


def pack_kernel(out_w, gu_w, down_w, a_ref, b_ref):
    a_ref[:, 0:D] = out_w[...].astype(bf16)
    a_ref[:, D:PAD_D] = jnp.zeros((ROWS, PAD_D - D), bf16)
    for half in range(2):
        for s in range(SHARDS):
            for i in range(3):
                col = (half * 12 + s * 3 + i) * LANE
                block = gu_w[:, col : col + LANE].astype(bf16)
                if i < 2:
                    to = PAD_D + ((half * 4 + s) * 2 + i) * LANE
                    a_ref[:, to : to + LANE] = block
                else:
                    to = (half * 4 + s) * LANE
                    b_ref[:, to : to + LANE] = block
    for i in range(3):
        ref, to = (a_ref, PAD_D + 2048 + i * PAD_D) if i < 2 else (b_ref, 1024)
        ref[:, to : to + PAD_D] = jnp.zeros((ROWS, PAD_D), bf16)
        ref[0:LANE, to : to + D] = down_w[i * LANE : (i + 1) * LANE, :].astype(bf16)


A_COLS = PAD_D + 2048 + 2 * PAD_D
B_COLS = 1024 + PAD_D


def pack_weights(w_out, w_gu, w_down):
    return call(
        pack_kernel,
        (sds((ROWS, A_COLS), bf16), sds((ROWS, B_COLS), bf16)),
        [VM] * 3,
        (VM, VM),
        [],
        "pack_weights",
        0,
        5e6,
    )(w_out, w_gu, w_down)


def fill_bias(start_ref, bias_ref, tokens):
    for i in range(tokens // TB):
        t0 = i * TB
        u0 = max(0, t0 - WINDOW)
        count = t0 + TB - u0
        first = start_ref[0:1, t0 : t0 + TB]
        token = lax.broadcasted_iota(jnp.int32, (1, TB), 1) + t0

        def block(n, carry, u0=u0, first=first, token=token, i=i):
            key = lax.broadcasted_iota(jnp.int32, (LANE, TB), 0) + (u0 + n * LANE)
            keep = (key >= first) & (key <= token)
            rows = pl.ds(pl.multiple_of(n * LANE, LANE), LANE)
            bias_ref[i, rows, :] = jnp.where(keep, 0.0, -1e30).astype(f32)
            return carry

        lax.fori_loop(0, count // LANE, block, 0)


def attend_kernel(
    scal, x_ref, w0, w1, w2, w3, cos_ref, sin_ref, start_ref,
    h1t_ref, qt_ref, kt_ref, kv_ref, ot_ref, log_ref, gain_ref,
    wq, wt, h1, vt, bias, sems,
):
    tokens = x_ref.shape[0]
    me = scal[0]
    copies = []
    for n, piece in enumerate((w0, w1, w2, w3)):
        rows = pl.ds(pl.multiple_of((me ^ PEERS[n]) * ROWS, 16), ROWS)
        copies.append(pltpu.make_async_copy(piece, wq.at[rows, :], sems.at[n]))
    for c in copies:
        c.start()
    fill_bias(start_ref, bias, tokens)
    for c in copies:
        c.wait()
    tail = wq[:, 1024 - LANE : 1024].astype(f32)
    tail_t = tail.T
    gains = tail_t[64:72, :]
    gain_ref[...] = gains
    gain_one = gains[0:1, :]

    def norm(b, carry):
        rows = pl.ds(pl.multiple_of(b * LANE, LANE), LANE)
        x = x_ref[rows, :].astype(f32)
        inv = lax.rsqrt(jnp.mean(x * x, -1, keepdims=True) + eps_norm)
        h1[rows, :] = ((x * inv) * gain_one).astype(bf16)
        return carry

    lax.fori_loop(0, tokens // LANE, norm, 0)
    h1t_ref[...] = h1[...].T
    wt[...] = wq[...].T

    def project(j, carry):
        cos = cos_ref[...]
        sin = sin_ref[...]
        h1t = h1t_ref[...]
        for g in range(GROUP):
            rows = pl.ds(pl.multiple_of((j * GROUP + g) * HD, HD), HD)
            q = nn(wt[rows, :], h1t)
            lo, hi = q[:HALF], q[HALF:]
            qt_ref[j, g * HD : g * HD + HALF, :] = (lo * cos - hi * sin).astype(bf16) * 0.125
            qt_ref[j, g * HD + HALF : (g + 1) * HD, :] = (hi * cos + lo * sin).astype(bf16) * 0.125
        k = nn(wt[pl.ds(pl.multiple_of(D + j * HD, HD), HD), :], h1t)
        v = nn(wt[pl.ds(pl.multiple_of(D + KV * HD + j * HD, HD), HD), :], h1t).astype(bf16)
        lo, hi = k[:HALF], k[HALF:]
        kr = jnp.concatenate([lo * cos - hi * sin, hi * cos + lo * sin], 0).astype(bf16)
        kt_ref[j] = kr
        vt[j] = v
        kv_ref[j] = jnp.concatenate([kr, v], 0).T
        return carry

    lax.fori_loop(0, KV, project, 0)
    blank = jnp.zeros((HD, TB), bf16)
    log_ref[...] = jnp.zeros(log_ref.shape, f32)

    def group(j, carry):
        for i in range(tokens // TB):
            t0 = i * TB
            u0 = max(0, t0 - WINDOW)
            count = t0 + TB - u0
            keys = kv_ref[j, u0 : u0 + count, :]
            vals = vt[j, :, u0 : u0 + count]
            for g in range(GROUP):
                q = qt_ref[j, g * HD : (g + 1) * HD, t0 : t0 + TB]
                s = nn(keys, jnp.concatenate([q, blank], 0)) + bias[i, :count, :]
                top = jnp.max(s, 0, keepdims=True)
                e = jnp.exp(s - top)
                total = jnp.sum(e, 0, keepdims=True)
                o = nn(vals, e.astype(bf16))
                ot_ref[j, g * HD : (g + 1) * HD, t0 : t0 + TB] = (o / total).astype(bf16)
                log_ref[j, g : g + 1, t0 : t0 + TB] = top + jnp.log(total)
        return carry

    lax.fori_loop(0, KV, group, 0)


def attend(scal, hidden, pieces, cos, sin, start):
    t = hidden.shape[0]
    return call(
        attend_kernel,
        (
            sds((D, t), bf16),
            sds((KV, GROUP * HD, t), bf16),
            sds((KV, HD, t), bf16),
            sds((KV, t, 2 * HD), bf16),
            sds((KV, GROUP * HD, t), bf16),
            sds((KV, 8, t), f32),
            sds((8, D), f32),
        ),
        [SM, VM] + [ANY] * 4 + [VM] * 3,
        tuple([VM] * 7),
        [
            pltpu.VMEM((D, 1024), bf16),
            pltpu.VMEM((1024, D), bf16),
            pltpu.VMEM((t, D), bf16),
            pltpu.VMEM((KV, HD, t), bf16),
            pltpu.VMEM((t // TB, WINDOW + TB, TB), f32),
            pltpu.SemaphoreType.DMA((4,)),
        ],
        "attend",
        4e9,
        10e6,
    )(scal, hidden, *pieces, cos, sin, start)


def attend_back_kernel(
    qt_ref, kt_ref, kv_ref, dot_ref, ot_ref, log_ref, cos_ref, sin_ref, start_ref, dp_ref,
    bias, dk, dv, drow,
):
    tokens = kv_ref.shape[1]
    fill_bias(start_ref, bias, tokens)
    dk[...] = jnp.zeros(dk.shape, f32)
    dv[...] = jnp.zeros(dv.shape, f32)
    for g in range(GROUP):
        rows = slice(g * HD, (g + 1) * HD)
        drow[g : g + 1, :] = jnp.sum(dot_ref[0, rows, :].astype(f32) * ot_ref[0, rows, :].astype(f32), 0, keepdims=True)
    blank = jnp.zeros((HD, TB), bf16)
    for i in range(tokens // TB):
        t0 = i * TB
        u0 = max(0, t0 - WINDOW)
        count = t0 + TB - u0
        cos = cos_ref[:, t0 : t0 + TB]
        sin = sin_ref[:, t0 : t0 + TB]
        for g in range(GROUP):
            keys = kv_ref[0, u0 : u0 + count, :]
            rows = slice(g * HD, (g + 1) * HD)
            q = qt_ref[0, rows, t0 : t0 + TB]
            do = dot_ref[0, rows, t0 : t0 + TB]
            s = nn(keys, jnp.concatenate([q, blank], 0)) + bias[i, :count, :]
            p = jnp.exp(s - log_ref[0, g : g + 1, t0 : t0 + TB])
            dp = nn(keys, jnp.concatenate([blank, do], 0))
            ds = (p * (dp - drow[g : g + 1, t0 : t0 + TB])).astype(bf16)
            dq = nn(kt_ref[0, :, u0 : u0 + count], ds) * 0.125
            lo, hi = dq[:HALF], dq[HALF:]
            dp_ref[g * HD : g * HD + HALF, t0 : t0 + TB] = (lo * cos + hi * sin).astype(bf16)
            dp_ref[g * HD + HALF : (g + 1) * HD, t0 : t0 + TB] = (hi * cos - lo * sin).astype(bf16)
            dk[:, u0 : u0 + count] += nt(q, ds)
            dv[:, u0 : u0 + count] += nt(do, p.astype(bf16))
    cos = cos_ref[...]
    sin = sin_ref[...]
    lo, hi = dk[:HALF], dk[HALF:]
    base = GROUP * HD
    dp_ref[base : base + HALF, :] = (lo * cos + hi * sin).astype(bf16)
    dp_ref[base + HALF : base + HD, :] = (hi * cos - lo * sin).astype(bf16)
    dp_ref[base + HD : base + 2 * HD, :] = dv[...].astype(bf16)


def attend_back(j, qt, kt, kv, dot, ot, log, cos, sin, start):
    t = kv.shape[1]

    def part(shape):
        return pl.BlockSpec((1,) + shape, lambda n: (j,) + (0,) * len(shape))

    def full(shape):
        return pl.BlockSpec(shape, lambda n: (0,) * len(shape))

    return pl.pallas_call(
        attend_back_kernel,
        grid=(1,),
        out_shape=sds(((GROUP + 2) * HD, t), bf16),
        in_specs=[
            part((GROUP * HD, t)), part((HD, t)), part((t, 2 * HD)), part((GROUP * HD, t)), part((GROUP * HD, t)),
            part((8, t)), full((HALF, t)), full((HALF, t)), full((1, t)),
        ],
        out_specs=full(((GROUP + 2) * HD, t)),
        scratch_shapes=[
            pltpu.VMEM((t // TB, WINDOW + TB, TB), f32),
            pltpu.VMEM((HD, t), f32),
            pltpu.VMEM((HD, t), f32),
            pltpu.VMEM((8, t), f32),
        ],
        name="attend_back",
        cost_estimate=pl.CostEstimate(flops=int(5e9), bytes_accessed=int(3e6), transcendentals=0),
        compiler_params=pltpu.CompilerParams(vmem_limit_bytes=40 * 1024 * 1024),
    )(qt, kt, kv, dot, ot, log, cos, sin, start)


def rel_index(me, s):
    rel = me ^ s
    return (rel & 1) * 2 + (rel >> 1)


def load_chunk(me, pieces, wgu, wd, gu_at, down_at, n, sems):
    copies = []
    for k, piece in enumerate(pieces):
        s = me ^ PEERS[k]
        rows = pl.ds(pl.multiple_of(s * ROWS, 16), ROWS)
        copies.append(pltpu.make_async_copy(piece.at[:, gu_at : gu_at + n * 1024], wgu.at[rows, :], sems.at[k]))
        for i in range(n):
            rows = pl.ds(pl.multiple_of((s * n + i) * LANE, LANE), LANE)
            at = down_at + i * PAD_D
            copies.append(
                pltpu.make_async_copy(piece.at[0:LANE, at : at + PAD_D], wd.at[rows, :], sems.at[4 + k * 2 + i])
            )
    return copies


def load_out(me, pieces, wout, sems):
    copies = []
    for k, piece in enumerate(pieces):
        rows = pl.ds(pl.multiple_of((me ^ PEERS[k]) * ROWS, 16), ROWS)
        copies.append(pltpu.make_async_copy(piece.at[:, 0:PAD_D], wout.at[rows, :], sems.at[12 + k]))
    return copies


def feed(n, first, tokens, h2, cot_ref, wgu, wd, hid, dgu, acc_ref, dh2_ref, acc_in=None, dh2_in=None):
    wide = n * 512
    step = 512

    def block(b, carry):
        rows = pl.ds(pl.multiple_of(b * TB, TB), TB)
        h = h2[rows, :]
        c = cot_ref[rows, :]
        for f in range(wide // step):
            gate = nn(h, wgu[:, f * step : (f + 1) * step])
            up = nn(h, wgu[:, wide + f * step : wide + (f + 1) * step])
            dh = nt(c, wd[f * step : (f + 1) * step, 0:D])
            sg = 1.0 / (1.0 + jnp.exp(-gate))
            act = gate * sg
            hid[rows, f * step : (f + 1) * step] = (act * up).astype(bf16)
            dgu[rows, f * step : (f + 1) * step] = (dh * up * (sg + act * (1.0 - sg))).astype(bf16)
            dgu[rows, wide + f * step : wide + (f + 1) * step] = (dh * act).astype(bf16)
        out = nn(hid[rows, :], wd[:, 0:D])
        back = nt(dgu[rows, :], wgu[...])
        if first:
            acc_ref[rows, :] = out
            dh2_ref[rows, :] = back
        else:
            acc_ref[rows, :] = acc_in[rows, :] + out
            dh2_ref[rows, :] = dh2_in[rows, :] + back
        return carry

    lax.fori_loop(0, tokens // TB, block, 0)


def feed_grads(n, me, mp, h2t, cott, hid, dgu, packed):
    def gate_up(p, carry):
        cols = pl.ds(pl.multiple_of(p * n * LANE, LANE), n * LANE)
        g = nn(h2t[...], dgu[:, cols]).astype(bf16)
        for s in range(SHARDS):
            for i in range(n):
                packed[rel_index(me, s), p ^ mp, i * SLAB : i * SLAB + ROWS, :] = g[
                    s * ROWS : (s + 1) * ROWS, i * LANE : (i + 1) * LANE
                ]
        return carry

    lax.fori_loop(0, PIECES, gate_up, 0)

    def down(s, carry):
        cols = pl.ds(pl.multiple_of(s * n * LANE, LANE), n * LANE)
        g = nn(cott[...], hid[:, cols]).astype(bf16)
        for p in range(PIECES):
            for i in range(n):
                packed[rel_index(me, s), p ^ mp, i * SLAB + ROWS : (i + 1) * SLAB, :] = g[
                    p * DROWS : (p + 1) * DROWS, i * LANE : (i + 1) * LANE
                ]
        return carry

    lax.fori_loop(0, SHARDS, down, 0)


def emit(packed, keep_ref, send_ref, sems):
    one = pltpu.make_async_copy(packed.at[2:4], send_ref, sems.at[16])
    two = pltpu.make_async_copy(packed.at[0:2], keep_ref, sems.at[17])
    one.start()
    two.start()
    one.wait()
    two.wait()


def feed_a_kernel(
    scal, ot_ref, x_ref, cot_ref, gain_ref, p0, p1, p2, p3,
    keep_ref, send_ref, y1_ref, acc_ref, dh2_ref, h2_ref, h2t_ref, cott_ref,
    wout, wgu, wd, hid, dgu, packed, sems,
):
    tokens = x_ref.shape[0]
    me, mp = scal[0], scal[1]
    pieces = (p0, p1, p2, p3)
    early = load_out(me, pieces, wout, sems)
    later = load_chunk(me, pieces, wgu, wd, PAD_D, PAD_D + 2048, 2, sems)
    for c in early + later:
        c.start()
    cott_ref[...] = cot_ref[...].T
    gain = gain_ref[1:2, :]
    for c in early:
        c.wait()

    def middle(b, carry):
        rows = pl.ds(pl.multiple_of(b * TB, TB), TB)
        o = ot_ref[:, rows].T
        y = x_ref[rows, :].astype(f32) + nn(o, wout[:, 0:D])
        y1_ref[rows, :] = y
        inv = lax.rsqrt(jnp.mean(y * y, -1, keepdims=True) + eps_norm)
        h2_ref[rows, :] = ((y * inv) * gain).astype(bf16)
        return carry

    lax.fori_loop(0, tokens // TB, middle, 0)
    h2t_ref[...] = h2_ref[...].T
    for c in later:
        c.wait()
    feed(2, True, tokens, h2_ref, cot_ref, wgu, wd, hid, dgu, acc_ref, dh2_ref)
    feed_grads(2, me, mp, h2t_ref, cott_ref, hid, dgu, packed)
    emit(packed, keep_ref, send_ref, sems)


def feed_a(scal, ot, hidden, cot, gains, pieces):
    t = hidden.shape[0]
    group = sds((2, PIECES, 2 * SLAB, LANE), bf16)
    return call(
        feed_a_kernel,
        (
            group, group, sds((t, D), f32), sds((t, D), f32), sds((t, D), f32),
            sds((t, D), bf16), sds((D, t), bf16), sds((D, t), bf16),
        ),
        [SM] + [VM] * 4 + [ANY] * 4,
        (ANY, ANY) + tuple([VM] * 6),
        [
            pltpu.VMEM((D, PAD_D), bf16),
            pltpu.VMEM((D, 2048), bf16),
            pltpu.VMEM((1024, PAD_D), bf16),
            pltpu.VMEM((t, 1024), bf16),
            pltpu.VMEM((t, 2048), bf16),
            pltpu.VMEM((4, PIECES, 2 * SLAB, LANE), bf16),
            pltpu.SemaphoreType.DMA((18,)),
        ],
        "feed_a",
        12e9,
        20e6,
    )(scal, ot, hidden, cot, gains, *pieces)


def feed_b_kernel(
    scal, ot_ref, cot_ref, gain_ref, y1_ref, acc_in, dh2_in, h2_ref, h2t_ref, cott_ref,
    a0, a1, a2, a3, p0, p1, p2, p3,
    keep_ref, send_ref, out_ref, dy1_ref, dot_ref,
    wout, wgu, wd, hid, dgu, packed, da, acc, dh2, go, sems,
):
    tokens = cot_ref.shape[0]
    me, mp = scal[0], scal[1]
    later = load_out(me, (a0, a1, a2, a3), wout, sems)
    early = load_chunk(me, (p0, p1, p2, p3), wgu, wd, 0, 1024, 1, sems)
    for c in early + later:
        c.start()
    for c in early:
        c.wait()
    feed(1, False, tokens, h2_ref, cot_ref, wgu, wd, hid, dgu, acc, dh2, acc_in, dh2_in)
    gain = gain_ref[1:2, :]

    def close(b, carry):
        rows = pl.ds(pl.multiple_of(b * LANE, LANE), LANE)
        y = y1_ref[rows, :]
        out_ref[rows, :] = (y + acc[rows, :]).astype(bf16)
        inv = lax.rsqrt(jnp.mean(y * y, -1, keepdims=True) + eps_norm)
        n2 = y * inv
        e2 = dh2[rows, :] * gain
        dy = cot_ref[rows, :].astype(f32) + inv * (e2 - n2 * jnp.mean(e2 * n2, -1, keepdims=True))
        dy1_ref[rows, :] = dy
        da[rows, :] = dy.astype(bf16)
        return carry

    lax.fori_loop(0, tokens // LANE, close, 0)
    for c in later:
        c.wait()
    for j in range(KV):
        lo = j * GROUP * HD
        dot_ref[j] = nt(wout[lo : lo + GROUP * HD, 0:D], da[...]).astype(bf16)
    feed_grads(1, me, mp, h2t_ref, cott_ref, hid, dgu, packed)
    go[:, 0:D] = nn(ot_ref[...], da[...]).astype(bf16)
    go[:, D:PAD_D] = jnp.zeros((D, PAD_D - D), bf16)
    for s in range(SHARDS):
        for p in range(PIECES):
            for at, k, row, rows in OUT_RUNS[p]:
                packed[rel_index(me, s), p ^ mp, SLAB + at : SLAB + at + rows, :] = go[
                    s * ROWS + row : s * ROWS + row + rows, k * LANE : (k + 1) * LANE
                ]
            used = sum([r[3] for r in OUT_RUNS[p]])
            if used < OUT_ROWS:
                packed[rel_index(me, s), p ^ mp, SLAB + used : SLAB + OUT_ROWS, :] = jnp.zeros(
                    (OUT_ROWS - used, LANE), bf16
                )
    emit(packed, keep_ref, send_ref, sems)


def feed_b(scal, ot, cot, gains, y1, acc, dh2, h2, h2t, cott, pieces_a, pieces_b):
    t = cot.shape[0]
    group = sds((2, PIECES, SLAB + OUT_ROWS, LANE), bf16)
    return call(
        feed_b_kernel,
        (group, group, sds((t, D), bf16), sds((t, D), f32), sds((KV, GROUP * HD, t), bf16)),
        [SM] + [VM] * 9 + [ANY] * 8,
        (ANY, ANY) + tuple([VM] * 3),
        [
            pltpu.VMEM((D, PAD_D), bf16),
            pltpu.VMEM((D, 1024), bf16),
            pltpu.VMEM((512, PAD_D), bf16),
            pltpu.VMEM((t, 512), bf16),
            pltpu.VMEM((t, 1024), bf16),
            pltpu.VMEM((4, PIECES, SLAB + OUT_ROWS, LANE), bf16),
            pltpu.VMEM((t, D), bf16),
            pltpu.VMEM((t, D), f32),
            pltpu.VMEM((t, D), f32),
            pltpu.VMEM((D, PAD_D), bf16),
            pltpu.SemaphoreType.DMA((18,)),
        ],
        "feed_b",
        9e9,
        20e6,
    )(scal, ot, cot, gains, y1, acc, dh2, h2, h2t, cott, *pieces_a, *pieces_b)


def join_rows(parts, dp):
    for j, part in enumerate(parts):
        dp[j * 192 : (j + 1) * 192, :] = part[0:192, :]
        dp[D + j * HD : D + (j + 1) * HD, :] = part[192:256, :]
        dp[D + 192 + j * HD : D + 192 + (j + 1) * HD, :] = part[256:320, :]
    dp[QKV:, :] = jnp.zeros((dp.shape[0] - QKV, dp.shape[1]), bf16)


def grad_qkv_kernel(scal, h1t_ref, d0, d1, d2, keep_ref, send_ref, dp, packed, sems):
    me, mp = scal[0], scal[1]
    join_rows((d0, d1, d2), dp)

    def piece(p, carry):
        rows = pl.ds(pl.multiple_of(p * LANE, LANE), LANE)
        g = nt(h1t_ref[...], dp[rows, :]).astype(bf16)
        for s in range(SHARDS):
            packed[rel_index(me, s), p ^ mp] = g[s * ROWS : (s + 1) * ROWS, :]
        return carry

    lax.fori_loop(0, PIECES, piece, 0)
    emit(packed, keep_ref, send_ref, sems)


def grad_qkv_call(scal, h1t, parts):
    t = h1t.shape[1]
    group = sds((2, PIECES, ROWS, LANE), bf16)
    return call(
        grad_qkv_kernel,
        (group, group),
        [SM] + [VM] * 4,
        (ANY, ANY),
        [
            pltpu.VMEM((1024, t), bf16),
            pltpu.VMEM((4, PIECES, ROWS, LANE), bf16),
            pltpu.SemaphoreType.DMA((18,)),
        ],
        "grad_qkv",
        1.2e9,
        5e6,
    )(scal, h1t, *parts)


def grad_input_kernel(scal, x_ref, dy1_ref, gain_ref, d0, d1, d2, w0, w1, w2, w3, out_ref, wq, dp, dht, sems):
    tokens = x_ref.shape[0]
    me = scal[0]
    copies = []
    for n, piece in enumerate((w0, w1, w2, w3)):
        rows = pl.ds(pl.multiple_of((me ^ PEERS[n]) * ROWS, 16), ROWS)
        copies.append(pltpu.make_async_copy(piece, wq.at[rows, :], sems.at[n]))
    for c in copies:
        c.start()
    join_rows((d0, d1, d2), dp)
    for c in copies:
        c.wait()
    gain = gain_ref[0:1, :]

    def block(b, carry):
        rows = pl.ds(pl.multiple_of(b * TB, TB), TB)
        dh = nn(wq[...], dp[:, rows]).T
        x = x_ref[rows, :].astype(f32)
        inv = lax.rsqrt(jnp.mean(x * x, -1, keepdims=True) + eps_norm)
        n1 = x * inv
        e1 = dh * gain
        dx = dy1_ref[rows, :] + inv * (e1 - n1 * jnp.mean(e1 * n1, -1, keepdims=True))
        out_ref[rows, :] = dx.astype(bf16)
        return carry

    lax.fori_loop(0, tokens // TB, block, 0)


def grad_input_call(scal, hidden, dy1, gains, parts, pieces):
    t = hidden.shape[0]
    return call(
        grad_input_kernel,
        sds((t, D), bf16),
        [SM] + [VM] * 6 + [ANY] * 4,
        VM,
        [
            pltpu.VMEM((D, 1024), bf16),
            pltpu.VMEM((1024, t), bf16),
            pltpu.VMEM((D, TB), f32),
            pltpu.SemaphoreType.DMA((4,)),
        ],
        "grad_input",
        1.2e9,
        8e6,
    )(scal, hidden, dy1, gains, *parts, *pieces)


def adam(w, m, v, g, rate, decay):
    m_new = beta_one * m + (1.0 - beta_one) * g
    v_new = beta_two * v + (1.0 - beta_two) * g * g
    mean_hat = m_new * (1.0 / (1.0 - beta_one**STEP))
    square_hat = v_new * (1.0 / (1.0 - beta_two**STEP))
    change = -rate * (mean_hat / (jnp.sqrt(square_hat) + adam_eps) + decay * w)
    return change, m_new, v_new


def put(refs, index, g, rate, decay):
    w, m, v, grad, new, nm, nv = refs
    grad[index] = g
    new[index], nm[index], nv[index] = adam(w[index], m[index], v[index], g, rate, decay)


def adam_feed_kernel(factor, scal, a0, a1, b0, b1, *refs):
    gu, down, out = [refs[k * 3 : k * 3 + 3] + refs[9 + k * 4 : 9 + k * 4 + 4] for k in range(3)]
    gain_sum = refs[21]
    gd, go = refs[22], refs[23]
    mp = scal[1]
    total = jnp.zeros((ROWS, LANE), f32)
    for d in range(PIECES):
        p = d ^ mp
        a = (a0, a1)[d // 4]
        b = (b0, b1)[d // 4]
        for i in range(3):
            ref, at = (a, i * SLAB) if i < 2 else (b, 0)
            g = ref[d % 4, at : at + ROWS, :].astype(f32) * factor
            cols = pl.ds(pl.multiple_of((3 * p + i) * LANE, LANE), LANE)
            put(gu, (slice(None), cols), g, rate_matrix, decay_weight)
            total = total + gu[0][:, cols].astype(bf16).astype(f32) * g
            rows = pl.ds(pl.multiple_of(p * DROWS, 8), DROWS)
            gd[i, rows, :] = ref[d % 4, at + ROWS : at + SLAB, :].astype(f32) * factor
        go[p] = b[d % 4, SLAB : SLAB + OUT_ROWS, :].astype(f32) * factor
    gain_sum[...] = jnp.broadcast_to(jnp.sum(total, 1, keepdims=True), (ROWS, LANE))
    for i in range(3):
        g = gd[i].T
        put(down, (slice(i * LANE, (i + 1) * LANE), slice(None)), g, rate_matrix, decay_weight)
    for p in range(PIECES):
        for at, k, row, rows in OUT_RUNS[p]:
            width = min(LANE, D - k * LANE)
            index = (slice(row, row + rows), slice(k * LANE, k * LANE + width))
            put(out, index, go[p, at : at + rows, 0:width], rate_matrix, decay_weight)


def adam_feed(factor, scal, a, b, gu, down, out):
    shapes = [sds(x[0].shape, f32) for x in (gu, down, out) for _ in range(4)]
    return call(
        functools.partial(adam_feed_kernel, factor),
        tuple(shapes) + (sds((ROWS, LANE), f32),),
        [SM] + [VM] * 13,
        tuple([VM] * 13),
        [pltpu.VMEM((3, D, LANE), f32), pltpu.VMEM((PIECES, OUT_ROWS, LANE), f32)],
        "adam_feed",
        1e8,
        25e6,
    )(scal, *a, *b, *gu, *down, *out)


def adam_qkv_kernel(factor, scal, q0, q1, sum_ref, *refs):
    qkv = refs[0:3] + refs[6:10]
    gains = refs[3:6] + refs[10:14]
    wide = refs[14]
    mp = scal[1]
    for d in range(PIECES):
        cols = pl.ds(pl.multiple_of((d ^ mp) * LANE, LANE), LANE)
        wide[:, cols] = (q0, q1)[d // 4][d % 4].astype(f32) * factor
    g = wide[:, 0:QKV]
    put(qkv, (slice(None), slice(None)), g, rate_matrix, decay_weight)
    one = jnp.sum(qkv[0][...].astype(bf16).astype(f32) * g, 1, keepdims=True)
    lane = lax.broadcasted_iota(jnp.int32, (ROWS, LANE), 1)
    both = jnp.where(lane == 0, one, sum_ref[...]).T
    low = gains[0][...].astype(bf16).astype(f32)
    put(gains, (slice(None), slice(None)), both[0:2, :] / low, rate_gain, 0.0)


def adam_qkv(factor, scal, q, gain_sum, qkv, gains):
    shapes = [sds(x[0].shape, f32) for x in (qkv, gains) for _ in range(4)]
    return call(
        functools.partial(adam_qkv_kernel, factor),
        tuple(shapes),
        [SM] + [VM] * 9,
        tuple([VM] * 8),
        [pltpu.VMEM((ROWS, 1024), f32)],
        "adam_qkv",
        1e7,
        5e6,
    )(scal, *q, gain_sum, *qkv, *gains)


def swap(v, axis, size, bit):
    return lax.ppermute(v, axis, [(i, i ^ (1 << bit)) for i in range(size)])


def add(a, b):
    return (a.astype(f32) + b.astype(f32)).astype(bf16)


def after(v, other):
    return lax.optimization_barrier((v, other))[0]


def gather(w):
    far = swap(w, "shard", SHARDS, 1)
    near = swap(w, "shard", SHARDS, 0)
    return (w, far, near, swap(far, "shard", SHARDS, 0))


def reduce_group(keep, send, dp, x_first):
    rows = keep.shape[2]
    shape = (2, 2, 2, 2, rows, LANE)
    got = swap(send, "shard", SHARDS, 0).reshape(shape)
    own = keep.reshape(shape)
    hops = [("shard", SHARDS, 1, 0), ("dp", dp, 0, 1), ("dp", dp, 1, 2), ("dp", dp, 2, 3)]
    if x_first:
        hops = [hops[1], hops[0], hops[2], hops[3]]
    left = [0, 1, 2, 3]
    for axis, size, bit, dim in hops:
        at = left.index(dim)
        left.pop(at)
        away = lax.index_in_dim(own, 1, at, False), lax.index_in_dim(got, 1, at, False)
        stay = lax.index_in_dim(own, 0, at, False), lax.index_in_dim(got, 0, at, False)
        got = swap(add(*away), axis, size, bit)
        own = add(*stay)
    own = add(own, got)
    for bit in range(3, dp.bit_length() - 1):
        own = add(own, swap(own, "dp", dp, bit))
    own = own[None]
    for bit in (2, 1):
        own = jnp.concatenate([own, swap(own, "dp", dp, bit)], 0)
    return own, swap(own, "dp", dp, 0)


def body(
    dp,
    hidden_in, cotangent, lengths,
    w_qkv, w_out, w_gu, w_down, norm_gains,
    moment_qkv, moment_out, moment_gu, moment_down, moment_gains,
    square_qkv, square_out, square_gu, square_down, square_gains,
):
    tokens = hidden_in.shape[0]
    shard = lax.axis_index("shard")
    rank = lax.axis_index("dp")
    label = (rank & 1) * 4 + ((rank >> 1) & 1) * 2 + ((rank >> 2) & 1)
    scal = jnp.stack([shard, label]).astype(jnp.int32)

    pack_q = jnp.concatenate(
        [w_qkv.astype(bf16), norm_gains.T.astype(bf16), jnp.zeros((ROWS, 1024 - QKV - 2), bf16)], 1
    )
    pieces_q = gather(pack_q)
    pack_a, pack_b = pack_weights(w_out, w_gu, w_down)
    pieces_a = gather(after(pack_a, pieces_q[1]))
    pieces_b = gather(after(pack_b, pieces_a[1]))

    ends = jnp.cumsum(lengths[0])
    token = jnp.arange(tokens, dtype=jnp.int32)
    start = jnp.sum(jnp.where(token[None, :] >= ends[:, None], lengths[0][:, None], 0), 0, keepdims=True)
    start = start.astype(jnp.int32)
    inverse = rope_base ** (-(jnp.arange(HALF, dtype=f32) * 2.0) / HD)
    angles = inverse[:, None] * (token[None, :] - start).astype(f32)
    cos, sin = jnp.cos(angles), jnp.sin(angles)

    h1t, qt, kt, kv, ot, log, gains = attend(scal, hidden_in, pieces_q, cos, sin, start)
    flat_ot = ot.reshape(D, tokens)
    keep_a, send_a, y1, acc, dh2, h2, h2t, cott = feed_a(scal, flat_ot, hidden_in, cotangent, gains, pieces_a)
    keep_b, send_b, output, dy1, dot = feed_b(
        scal, flat_ot, cotangent, gains, y1, acc, dh2, h2, h2t, cott, pieces_a, pieces_b
    )
    sum_a = reduce_group(keep_a, send_a, dp, False)
    sum_b = reduce_group(keep_b, send_b, dp, True)
    parts = [attend_back(j, qt, kt, kv, dot, ot, log, cos, sin, start) for j in range(KV)]
    keep_c, send_c = grad_qkv_call(scal, h1t, parts)
    sum_c = reduce_group(keep_c, send_c, dp, False)
    grad_input = grad_input_call(scal, hidden_in, dy1, gains, parts, pieces_q)

    factor = 1.0 / math.sqrt(dp * SHARDS * tokens)
    (
        grad_gu, new_gu, new_moment_gu, new_square_gu,
        grad_down, new_down, new_moment_down, new_square_down,
        grad_out, new_out, new_moment_out, new_square_out,
        gain_sum,
    ) = adam_feed(
        factor, scal, sum_a, sum_b,
        (w_gu, moment_gu, square_gu), (w_down, moment_down, square_down), (w_out, moment_out, square_out),
    )
    (
        grad_qkv, new_qkv, new_moment_qkv, new_square_qkv,
        grad_gains, new_gains, new_moment_gains, new_square_gains,
    ) = adam_qkv(
        factor, scal, sum_c, gain_sum, (w_qkv, moment_qkv, square_qkv), (norm_gains, moment_gains, square_gains)
    )
    return (
        output, grad_input,
        grad_qkv, grad_out, grad_gu, grad_down, grad_gains,
        new_qkv, new_out, new_gu, new_down, new_gains,
        new_moment_qkv, new_moment_out, new_moment_gu, new_moment_down, new_moment_gains,
        new_square_qkv, new_square_out, new_square_gu, new_square_down, new_square_gains,
    )


def solution(mesh):
    rows = P(("dp", "shard"), None)
    own = P("shard", None)
    gain = P(None, "shard")
    params = (own, own, own, own, gain)
    return jax.shard_map(
        functools.partial(body, mesh.shape["dp"]),
        mesh=mesh,
        in_specs=(rows, rows, rows) + params * 3,
        out_specs=(rows, rows) + params * 4,
        check_vma=False,
    )
```
